128 devices in a mesh: rows: 8 (over y, core), acts: 16 (over z, x).
Axes of the slice: x: 4, y: 4, z: 4, core: 2. Of those that a mesh axis runs over, the one named last changes fastest.
Arguments:
- features: bfloat16 [32768, 2048], P('rows'), may hold values from -6 to 80
- policy_weight: bfloat16 [2048, 4096], P(None, 'acts'), may hold values from -3 to 3
- reward_weight: bfloat16 [2048, 4096], P(None, 'acts'), may hold values from -1 to 1
- logged_action: int32 [32768], P('rows'), may hold values from 0 to 4095
- reward_level: int32 [32768], P('rows'), may hold values from 0 to 4
- logged_propensity: float32 [32768], P('rows'), may hold values from 9.765625e-05 to 0.0009765625
Outputs:
- policy_grad: float32 [2048, 4096], P(None, 'acts')
- reward_grad: float32 [2048, 4096], P(None, 'acts')
- row_value: float32 [32768], P('rows')
The draws below stay inside these ranges and needn't reach their ends.
All inputs are finite; a program needn't handle non-finite values.
Results may differ from the reference program's by a relative error of at most 0.015.
Values may be sent and summed in bfloat16 or wider, within the bound.
No kernel may reach another device: no remote copies, remote signals or barrier semaphores. Data moves between devices by JAX's collectives and lax.ppermute only.
A program may use at most 128 MiB of HBM per device.

```python
import math
import jax
import jax.numpy as jnp
import numpy as np
from jax import lax

D = 2048
ACTIONS = 4096
ROW_DEV = 4096
ROWS = 32768
N_ROWS = 8


def draw_features(key, part):
    own_key = jax.random.fold_in(key, 21)
    values = jnp.clip(jax.random.normal(own_key, (ROWS, D), jnp.float32), -6.0, 6.0)
    return values.astype(jnp.bfloat16)


def draw_policy_weight(key, part):
    own_key = jax.random.fold_in(key, 31)
    values = jnp.clip(jax.random.normal(own_key, (D, ACTIONS), jnp.float32), -6.0, 6.0) / jnp.sqrt(jnp.float32(D))
    return values.astype(jnp.bfloat16)


def draw_reward_weight(key, part):
    own_key = jax.random.fold_in(key, 41)
    scale = 1.0 / jnp.sqrt(jnp.float32(D))
    values = jnp.clip(jax.random.normal(own_key, (D, ACTIONS), jnp.float32), -6.0, 6.0) * scale
    shared = jnp.clip(jax.random.normal(jax.random.fold_in(key, 5), (D,), jnp.float32), -6.0, 6.0) * scale
    return jnp.clip(values + shared[:, None], -1.0, 1.0).astype(jnp.bfloat16)


def plant(values, rng, smallest, high):
    shape = values.shape
    place = [jax.random.randint(jax.random.fold_in(rng, axis), (), 0, shape[axis]) for axis in range(len(shape))]
    values = values.at[tuple(place)].set(smallest)
    longest = shape.index(max(shape))
    place[longest] = (place[longest] + 1) % shape[longest]
    return values.at[tuple(place)].set(high)


def level_of(key, dims, shards, least, top_value):
    loudness, own = 1.0, jax.random.fold_in(key, 6)
    for position, shards_of in shards:
        draws = jnp.exp(jax.random.uniform(jax.random.fold_in(own, position), (shards_of,), jnp.float32, least / len(shards), top_value / len(shards)))
        loudness = loudness * jnp.repeat(draws, dims[position] // shards_of).reshape([-1 if axis == position else 1 for axis in range(len(dims))])
    return loudness


def cumulative_ranks(amount, skew):
    loads = [(1 << 20) // math.isqrt(standing ** skew) + 1 for standing in range(1, amount + 1)]
    width = 1 + sum(loads) // (1 << 30)
    return np.cumsum(np.array([max(1, weight // width) for weight in loads]))


def skewed_ids(key, extent, amount, skew):
    grid = cumulative_ranks(amount, skew)
    pick = jax.random.randint(jax.random.fold_in(key, 1), extent, 0, int(grid[amount - 1]))
    standing = jnp.searchsorted(jnp.asarray(grid, jnp.int32), pick, side="right")
    return jax.random.permutation(jax.random.fold_in(key, 2), amount)[standing].astype(jnp.int32)


def setup_inputs(seed: int = 0) -> dict:
    arg_keys = jax.random.split(jax.random.key(seed), 7)
    features = draw_features(jax.random.fold_in(arg_keys[6], 71), 0)
    policy_weight = draw_policy_weight(jax.random.fold_in(arg_keys[6], 71), 0)
    reward_weight = draw_reward_weight(jax.random.fold_in(arg_keys[6], 71), 0)
    logged_action = plant(skewed_ids(arg_keys[3], (ROWS,), ACTIONS, 2), jax.random.fold_in(arg_keys[3], 3), 0, ACTIONS - 1).astype(jnp.int32)
    reward_level = plant(jax.random.randint(arg_keys[4], (ROWS,), 0, 5), jax.random.fold_in(arg_keys[4], 1), 0, 4).astype(jnp.int32)
    logged_propensity = jnp.clip(jnp.exp(math.log(0.0009765625) - 2.3025851 * jax.random.uniform(arg_keys[5], (ROWS,), jnp.float32) ** level_of(arg_keys[5], (ROWS,), ((0, 8),), -0.2, 0.2)), 9.765625145519152e-05, 0.0009765625)
    return dict(features=features, policy_weight=policy_weight, reward_weight=reward_weight, logged_action=logged_action, reward_level=reward_level, logged_propensity=logged_propensity)


def reference(features, policy_weight, reward_weight, logged_action, reward_level, logged_propensity):
    scores = jnp.dot(features, policy_weight, preferred_element_type=jnp.float32)
    predicted = jnp.dot(features, reward_weight, preferred_element_type=jnp.float32)
    largest = jnp.max(scores, axis=1, keepdims=True)
    exponent = jnp.exp(scores - largest)
    row_total = jnp.sum(exponent, axis=1)
    weighted = jnp.sum(exponent * predicted, axis=1)
    columns = jnp.arange(ACTIONS, dtype=jnp.int32)
    onehot = logged_action[:, None] == columns[None, :]
    picked_exp = jnp.sum(jnp.where(onehot, exponent, jnp.float32(0.0)), axis=1)
    picked_pred = jnp.sum(jnp.where(onehot, predicted, jnp.float32(0.0)), axis=1)
    payoff = reward_level.astype(jnp.float32) * 0.25
    probability = exponent / row_total[:, None]
    mean_pred = weighted / row_total
    importance = picked_exp / row_total / logged_propensity
    corrected = importance * (payoff - picked_pred)
    row_value = mean_pred + corrected
    policy_term = (probability * (predicted - mean_pred[:, None])
                   + corrected[:, None] * (onehot.astype(jnp.float32) - probability)).astype(jnp.bfloat16)
    reward_term = jnp.where(onehot, predicted - payoff[:, None], jnp.float32(0.0)).astype(jnp.bfloat16)
    both_terms = jnp.concatenate((policy_term, reward_term), axis=1)
    grouped_feat = features.reshape(N_ROWS, ROW_DEV, D).astype(jnp.float32)
    grouped_terms = both_terms.reshape(N_ROWS, ROW_DEV, 2 * ACTIONS).astype(jnp.float32)
    partial_grad = jnp.einsum("gnd,gna->gda", grouped_feat, grouped_terms, precision=lax.Precision.HIGHEST)
    rounded = lax.optimization_barrier(partial_grad.astype(jnp.bfloat16))
    summed = jnp.sum(rounded.astype(jnp.float32), axis=0)
    return summed[:, :ACTIONS], summed[:, ACTIONS:], row_value
```

```python
import jax
import jax.numpy as jnp
from jax import lax
from jax.sharding import PartitionSpec as P

N_ROWS = 8
N_ACTS = 16


def swap(x, axis, mask, size):
    return lax.ppermute(x, axis, [(i, i ^ mask) for i in range(size)])


def merge(mine, other):
    top = jnp.maximum(mine[0], other[0])
    a = jnp.exp(mine[0] - top)
    b = jnp.exp(other[0] - top)
    return jnp.stack(
        [
            top,
            mine[1] * a + other[1] * b,
            mine[2] * a + other[2] * b,
            mine[3] * a + other[3] * b,
            mine[4] + other[4],
        ]
    )


def reduce_groups(partial, steps):
    held = partial.astype(jnp.bfloat16)
    trail = []
    for mask, bit in steps:
        half = held.shape[0] // 2
        keep = lax.dynamic_slice_in_dim(held, bit * half, half)
        send = lax.dynamic_slice_in_dim(held, (1 - bit) * half, half)
        got = swap(send.astype(jnp.bfloat16), "rows", mask, N_ROWS)
        held = keep.astype(jnp.float32) + got.astype(jnp.float32)
        trail.append((mask, bit))
    held = held.astype(jnp.bfloat16)
    for mask, bit in reversed(trail):
        got = swap(held, "rows", mask, N_ROWS)
        first = jnp.where(bit == 0, held, got)
        second = jnp.where(bit == 0, got, held)
        held = jnp.concatenate((first, second), axis=0)
    return held.astype(jnp.float32)


def on_device(
    features, policy_weight, reward_weight, logged_action, reward_level, logged_propensity
):
    me = lax.axis_index("rows")
    core, y0, y1 = me & 1, (me >> 1) & 1, (me >> 2) & 1
    scores = jnp.dot(features, policy_weight, preferred_element_type=jnp.float32)
    predicted = jnp.dot(features, reward_weight, preferred_element_type=jnp.float32)
    act_block = scores.shape[1]
    payoff = reward_level.astype(jnp.float32) * 0.25
    columns = jnp.arange(act_block, dtype=jnp.int32) + lax.axis_index("acts") * act_block
    onehot = logged_action[:, None] == columns[None, :]
    zero = jnp.float32(0.0)

    top = jnp.max(scores, axis=1)
    exponent = jnp.exp(scores - top[:, None])
    stats = jnp.stack(
        [
            top,
            jnp.sum(exponent, axis=1),
            jnp.sum(exponent * predicted, axis=1),
            jnp.sum(jnp.where(onehot, exponent, zero), axis=1),
            jnp.sum(jnp.where(onehot, predicted, zero), axis=1),
        ]
    )
    reward_term = jnp.where(onehot, predicted - payoff[:, None], zero).astype(jnp.bfloat16)
    contract = (((0,), (0,)), ((), ()))
    reward_part = lax.dot_general(
        features, reward_term, contract, preferred_element_type=jnp.float32
    )
    for mask in (1, 3, 4, 12):
        stats = merge(stats, swap(stats, "acts", mask, N_ACTS))
    reward_grad = reduce_groups(reward_part, ((1, core), (2, y0 ^ y1), (6, y1)))

    largest, row_total, weighted, picked_exp, picked_pred = stats
    mean_pred = weighted / row_total
    importance = picked_exp / row_total / logged_propensity
    corrected = importance * (payoff - picked_pred)
    row_value = mean_pred + corrected
    probability = jnp.exp(scores - largest[:, None]) / row_total[:, None]
    policy_term = (
        probability * (predicted - mean_pred[:, None])
        + corrected[:, None] * (onehot.astype(jnp.float32) - probability)
    ).astype(jnp.bfloat16)
    policy_part = lax.dot_general(
        features, policy_term, contract, preferred_element_type=jnp.float32
    )
    policy_grad = reduce_groups(policy_part, ((1, core), (6, y1), (2, y0)))
    return (policy_grad, reward_grad, row_value)


def solution(mesh):
    return jax.shard_map(
        on_device,
        mesh=mesh,
        in_specs=(
            P("rows", None),
            P(None, "acts"),
            P(None, "acts"),
            P("rows"),
            P("rows"),
            P("rows"),
        ),
        out_specs=(P(None, "acts"), P(None, "acts"), P("rows")),
        check_vma=False,
    )
```

```python
import jax
import jax.numpy as jnp
from jax import lax
from jax.sharding import PartitionSpec as P

N_ROWS = 8
N_ACTS = 16


def swap(x, axis, mask, size):
    return lax.ppermute(x, axis, [(i, i ^ mask) for i in range(size)])


def merge(mine, other):
    top = jnp.maximum(mine[0], other[0])
    a = jnp.exp(mine[0] - top)
    b = jnp.exp(other[0] - top)
    return jnp.stack(
        [
            top,
            mine[1] * a + other[1] * b,
            mine[2] * a + other[2] * b,
            mine[3] * a + other[3] * b,
            mine[4] + other[4],
        ]
    )


def halve(held, step):
    mask, bit = step
    half = held.shape[0] // 2
    keep = lax.dynamic_slice_in_dim(held, bit * half, half)
    send = lax.dynamic_slice_in_dim(held, (1 - bit) * half, half)
    got = swap(send.astype(jnp.bfloat16), "rows", mask, N_ROWS)
    return keep.astype(jnp.float32) + got.astype(jnp.float32)


def double(held, step):
    mask, bit = step
    got = swap(held, "rows", mask, N_ROWS)
    first = jnp.where(bit == 0, held, got)
    second = jnp.where(bit == 0, got, held)
    return jnp.concatenate((first, second), axis=0)


def on_device(
    features, policy_weight, reward_weight, logged_action, reward_level, logged_propensity
):
    me = lax.axis_index("rows")
    core, y0, y1 = me & 1, (me >> 1) & 1, (me >> 2) & 1
    act_block = policy_weight.shape[1]
    weights = jnp.concatenate((policy_weight, reward_weight), axis=1)
    both = jnp.dot(features, weights, preferred_element_type=jnp.float32)
    scores, predicted = both[:, :act_block], both[:, act_block:]
    payoff = reward_level.astype(jnp.float32) * 0.25
    columns = jnp.arange(act_block, dtype=jnp.int32) + lax.axis_index("acts") * act_block
    onehot = logged_action[:, None] == columns[None, :]
    zero = jnp.float32(0.0)

    top = jnp.max(scores, axis=1)
    exponent = jnp.exp(scores - top[:, None])
    stats = jnp.stack(
        [
            top,
            jnp.sum(exponent, axis=1),
            jnp.sum(exponent * predicted, axis=1),
            jnp.sum(jnp.where(onehot, exponent, zero), axis=1),
            jnp.sum(jnp.where(onehot, predicted, zero), axis=1),
        ]
    )
    reward_term = jnp.where(onehot, predicted - payoff[:, None], zero).astype(jnp.bfloat16)
    contract = (((0,), (0,)), ((), ()))
    reward_part = lax.dot_general(
        reward_term, features, contract, preferred_element_type=jnp.float32
    )
    reward_steps = ((1, core), (2, y0 ^ y1), (6, y1))
    policy_steps = ((1, core), (6, y1), (2, y0))
    stats = merge(stats, swap(stats, "acts", 1, N_ACTS))
    reward_held = reward_part.astype(jnp.bfloat16)
    for mask, step in zip((3, 4, 12), reward_steps):
        stats, reward_held = lax.optimization_barrier((stats, reward_held))
        stats = merge(stats, swap(stats, "acts", mask, N_ACTS))
        reward_held = halve(reward_held, step)
    stats, reward_held = lax.optimization_barrier((stats, reward_held.astype(jnp.bfloat16)))

    largest, row_total, weighted, picked_exp, picked_pred = stats
    mean_pred = weighted / row_total
    importance = picked_exp / row_total / logged_propensity
    corrected = importance * (payoff - picked_pred)
    row_value = mean_pred + corrected
    probability = jnp.exp(scores - largest[:, None]) / row_total[:, None]
    policy_term = (
        probability * (predicted - mean_pred[:, None])
        + corrected[:, None] * (onehot.astype(jnp.float32) - probability)
    ).astype(jnp.bfloat16)
    policy_part = lax.dot_general(
        policy_term, features, contract, preferred_element_type=jnp.float32
    )
    policy_held = policy_part.astype(jnp.bfloat16)
    for policy_step, reward_step in zip(policy_steps, reversed(reward_steps)):
        policy_held = halve(policy_held, policy_step)
        reward_held = double(reward_held, reward_step)
    policy_held = policy_held.astype(jnp.bfloat16)
    for step in reversed(policy_steps):
        policy_held = double(policy_held, step)
    return (policy_held.T.astype(jnp.float32), reward_held.T.astype(jnp.float32), row_value)


def solution(mesh):
    return jax.shard_map(
        on_device,
        mesh=mesh,
        in_specs=(
            P("rows", None),
            P(None, "acts"),
            P(None, "acts"),
            P("rows"),
            P("rows"),
            P("rows"),
        ),
        out_specs=(P(None, "acts"), P(None, "acts"), P("rows")),
        check_vma=False,
    )
```
